32 devices in a mesh: groups: 2 (over y), frame: 4 (over z), space: 4 (over x, core).
Axes of the slice: x: 2, y: 2, z: 4, core: 2. Of those that a mesh axis runs over, the one named last changes fastest.
Arguments:
- queries: float32 [16384, 128], P(('groups', 'frame', 'space')), parts along dimension 0, may hold values from -256 to 256
- keys: float32 [16384, 128], P(('groups', 'frame', 'space')), parts along dimension 0, may hold values from -8 to 8
- values: float32 [16384, 128], P(('groups', 'frame', 'space')), parts along dimension 0, may hold values from -6 to 6
- block_mask: int32 [4, 4], replicated, may hold values from 0 to 1, as said below
- partner_flags: int32 [4, 2, 2], replicated, may hold values 0 or 1
Outputs:
- attended: float32 [16384, 128], P(('groups', 'frame', 'space')), parts along dimension 0
The draws below stay inside these ranges and needn't reach their ends.
There are 2 independent parts, one for each index of `groups`. The reference program is written for one: setup_inputs(seed, part) draws one part's arguments, and reference() takes and returns one part's arrays. A program takes and returns all parts, laid end to end along the dimension named above; an argument that names none is the same for every part. Nothing has to cross between parts.
Inputs may be any that keep to these rules, and one draw needn't show every extreme that they name: block_mask[a, b] = 1 when a = b or |a - b| = 2, and block_mask[a, b] = 0 when |a - b| > 2. `partner_flags`: a partner outside frame groups 0 to 3 is never used, whatever its flag.
All inputs are finite; a program needn't handle non-finite values.
Results may differ from the reference program's by a relative error of at most 0.0003.
Values sent between devices are 32-bit elements; how exact they have to be, the bound alone decides.
No kernel may reach another device: no remote copies, remote signals or barrier semaphores. Data moves between devices by JAX's collectives and lax.ppermute only.
A program may use at most 64 MiB of HBM per device.

```python
import math
import jax
import jax.numpy as jnp
from jax import lax

HEAD = 128
TOK_DEV = 512
GROUPS = 4
BLOCKS = 4
LEVELS = 2
GROUP_TOKENS = 2048
TOKENS = 8192


def draw_pair(key):
    base = jax.random.fold_in(key, 41)
    first_key, second_key = jax.random.split(base, 2)
    keys_all = 1.6 * jax.random.truncated_normal(first_key, -5.0, 5.0, (TOKENS, HEAD), jnp.float32)
    query_all = 1.6 * jax.random.truncated_normal(second_key, -5.0, 5.0, (TOKENS, HEAD), jnp.float32)
    return (query_all, keys_all)


def draw_queries(key, part):
    return draw_pair(key)[0]


def draw_keys(key, part):
    return draw_pair(key)[1]


def draw_block_mask(key, part):
    random_bits = jax.random.randint(jax.random.fold_in(key, 11), (BLOCKS, BLOCKS), 0, 2)
    row_ids = lax.broadcasted_iota(jnp.int32, (BLOCKS, BLOCKS), 0)
    column_ids = lax.broadcasted_iota(jnp.int32, (BLOCKS, BLOCKS), 1)
    spread = jnp.abs(row_ids - column_ids)
    reach = BLOCKS // 2
    inner = jnp.where(spread < reach, random_bits, 0)
    return jnp.where((spread == 0) | (spread == reach), 1, inner).astype(jnp.int32)


def touch_ends(values, rng, low, high):
    index_at = [jax.random.randint(jax.random.fold_in(rng, axis), (), 0, length) for axis, length in enumerate(values.shape)]
    main_axis = values.shape.index(max(values.shape))
    next_to = index_at[:main_axis] + [(index_at[main_axis] + 1) % values.shape[main_axis]] + index_at[main_axis + 1:]
    return values.at[tuple(index_at)].set(low).at[tuple(next_to)].set(high)


def level_of(key, shape, pieces, low, top_value):
    def one(axis_at, parts):
        draws = jax.random.uniform(jax.random.fold_in(jax.random.fold_in(key, 6), axis_at), (parts,), jnp.float32, low / len(pieces), top_value / len(pieces))
        return jnp.repeat(jnp.exp(draws), shape[axis_at] // parts).reshape((-1,) + (1,) * (len(shape) - axis_at - 1))

    level = one(*pieces[0])
    for cut in pieces[1:]:
        level = level * one(*cut)
    return level


def gaussian(key, shape, scale, bound, cuts=(), kind=jnp.bfloat16):
    loudness = level_of(key, shape, cuts, -0.22, 0.18) if cuts else 1.0
    values = jax.random.normal(key, shape, jnp.float32) * scale * loudness
    return jnp.minimum(jnp.maximum(values, -bound), bound).astype(kind)


def setup_inputs(seed: int = 0, part: int = 0) -> dict:
    seeds = jax.random.split(jax.random.key(seed), 6)
    part_splits = jax.random.split(jax.random.fold_in(seeds[5], part), 6)
    return {
        "queries": draw_queries(jax.random.fold_in(jax.random.fold_in(seeds[5], part), 71), part),
        "keys": draw_keys(jax.random.fold_in(jax.random.fold_in(seeds[5], part), 71), part),
        "values": gaussian(part_splits[2], (TOKENS, HEAD), 1.0, 6.0, ((0, 16),), jnp.float32),
        "block_mask": draw_block_mask(jax.random.fold_in(seeds[5], 71), part),
        "partner_flags": touch_ends((jax.random.randint(seeds[4], (GROUPS, LEVELS, 2), 0, 4) < 3).astype(jnp.int32), jax.random.fold_in(seeds[4], 1), 0, 1),
    }


masked_score = -1e+30

def reference(queries, keys, values, block_mask, partner_flags):
    score_scale = 1.0 / math.sqrt(HEAD)
    query_blocks = queries.reshape(GROUPS, BLOCKS, TOK_DEV, HEAD)
    key_blocks = keys.reshape(GROUPS, BLOCKS, TOK_DEV, HEAD)
    value_blocks = values.reshape(GROUPS, BLOCKS, TOK_DEV, HEAD)

    def one_block(block_index):
        group_index = block_index // BLOCKS
        space_index = block_index % BLOCKS
        query_rows = query_blocks[group_index, space_index]
        key_parts = [key_blocks[group_index].reshape(GROUP_TOKENS, HEAD)]
        value_parts = [value_blocks[group_index].reshape(GROUP_TOKENS, HEAD)]
        allowed_parts = [jnp.repeat(block_mask[space_index] > 0, TOK_DEV)]
        for level_index in range(LEVELS):
            distance = 2 ** level_index
            for direction in range(2):
                partner = group_index - distance if direction == 0 else group_index + distance
                usable = (partner >= 0) & (partner < GROUPS) & (partner_flags[group_index, level_index, direction] > 0)
                clamped = jnp.clip(partner, 0, GROUPS - 1).astype(jnp.int32)
                key_parts.append(key_blocks[clamped, space_index])
                value_parts.append(value_blocks[clamped, space_index])
                allowed_parts.append(jnp.broadcast_to(usable, (TOK_DEV,)))
        all_keys = jnp.concatenate(key_parts, axis=0)
        all_values = jnp.concatenate(value_parts, axis=0)
        allowed = jnp.concatenate(allowed_parts, axis=0)
        scores = jnp.dot(query_rows, all_keys.T, precision=lax.Precision.HIGHEST, preferred_element_type=jnp.float32) * score_scale
        scores = jnp.where(allowed[None, :], scores, masked_score)
        row_max = lax.optimization_barrier(jnp.max(scores, axis=1, keepdims=True))
        weights = jnp.where(allowed[None, :], jnp.exp(scores - row_max), 0.0)
        row_total = lax.optimization_barrier(jnp.sum(weights, axis=1, keepdims=True))
        weighted = jnp.dot(weights, all_values, precision=lax.Precision.HIGHEST, preferred_element_type=jnp.float32)
        return weighted / row_total
    result = lax.map(one_block, jnp.arange(GROUPS * BLOCKS, dtype=jnp.int32))
    return result.reshape(TOKENS, HEAD)
```

```python
import functools
import math

import jax
import jax.numpy as jnp
from jax import lax
from jax.experimental import pallas as pl
from jax.experimental.pallas import tpu as pltpu
from jax.sharding import PartitionSpec as P


masked_score = -1e30
lane_count = 128
row_chunk = 256
call_blocks = 4
kernel_vmem = 24 * 2**20


def halves(x):
    high = x.astype(jnp.bfloat16)
    return high, (x - high.astype(jnp.float32)).astype(jnp.bfloat16)


def fold_lanes(x, op):
    folded = x[:, :lane_count]
    for start in range(lane_count, x.shape[1], lane_count):
        folded = op(folded, x[:, start : start + lane_count])
    return folded


def absorb(state, query_parts, key_parts, value_parts, enabled):
    scores = lax.dot_general(
        query_parts, key_parts, (((1,), (1,)), ((), ())), preferred_element_type=jnp.float32
    )
    block_max = jnp.max(fold_lanes(scores, jnp.maximum), axis=1, keepdims=True)
    if enabled is not None:
        block_max = jnp.where(enabled, block_max, masked_score)
    new_max = block_max if state is None else jnp.maximum(state[0], block_max)
    shift = new_max if enabled is None else jnp.where(enabled, new_max, -masked_score)
    weights = jnp.exp2(scores - shift)
    total = fold_lanes(weights, jnp.add)
    weights_high, weights_low = halves(weights)
    weighted = jnp.dot(weights_high, value_parts, preferred_element_type=jnp.float32)
    weighted += jnp.dot(weights_low, value_parts, preferred_element_type=jnp.float32)
    if state is None:
        return new_max, total, weighted
    factor = jnp.exp2(state[0] - new_max)
    return new_max, state[1] * factor + total, state[2] * factor + weighted


def partner_of(index, distance, parity):
    return jnp.where((index // distance) % 2 == parity, index + distance, index - distance)


def block_flag(which, block_mask, partner_flags):
    axis, distance, parity = which
    if axis == "space":
        index = lax.axis_index("space")
        partner = partner_of(index, distance, parity)
        inside = (partner >= 0) & (partner < block_mask.shape[1])
        return inside & (block_mask[index, jnp.clip(partner, 0, block_mask.shape[1] - 1)] > 0)
    index = lax.axis_index("frame")
    if axis == "relay":
        partner = jnp.where(index % 2 == parity, index + distance, index - distance)
    else:
        partner = partner_of(index, distance, parity)
    inside = (partner >= 0) & (partner < partner_flags.shape[0])
    upper = jnp.where(partner > index, 1, 0)
    return inside & (partner_flags[index, distance.bit_length() - 1, upper] > 0)


def attend_kernel(plan, first, last, block_mask, partner_flags, queries, *refs):
    position = 0
    key_parts = []
    value_parts = []
    enabled = []
    for kind, which in plan:
        if kind == "stacked":
            rows = refs[position].shape[0] // 2
            key_rows, value_rows = refs[position][:rows, :], refs[position][rows:, :]
            position += 1
        else:
            key_rows, value_rows = refs[position][...], refs[position + 1][...]
            position += 2
        flag = None if which is None else block_flag(which[0], block_mask, partner_flags)
        if kind == "either":
            other = block_flag(which[1], block_mask, partner_flags)
            key_rows = jnp.where(flag, key_rows, refs[position][...])
            value_rows = jnp.where(flag, value_rows, refs[position + 1][...])
            position += 2
            flag = flag | other
        key_high, key_low = halves(key_rows)
        key_parts.append(jnp.concatenate([key_high, key_high, key_low, key_low], axis=1))
        value_parts.append(jnp.concatenate(halves(value_rows), axis=1))
        enabled.append(flag)
    carried = () if first else refs[position : position + 3]
    outs = refs[position + len(carried) :]
    row_count, width = queries.shape
    chunk = min(row_chunk, row_count)
    score_scale = math.log2(math.e) / math.sqrt(width)
    for start in range(0, row_count, chunk):
        rows = slice(start, start + chunk)
        query_high, query_low = halves(queries[rows, :] * score_scale)
        query_parts = jnp.concatenate([query_high, query_low, query_high, query_low], axis=1)
        state = None if first else (carried[0][rows, :1], carried[1][rows, :], carried[2][rows, :])
        for index in range(len(plan)):
            state = absorb(state, query_parts, key_parts[index], value_parts[index], enabled[index])
        running_max, total, weighted = state
        if last:
            row_total = jnp.sum(total, axis=1, keepdims=True)
            outs[0][rows, :] = (weighted[:, :width] + weighted[:, width:]) / row_total
        else:
            outs[0][rows, :] = jnp.broadcast_to(running_max, (chunk, lane_count))
            outs[1][rows, :] = total
            outs[2][rows, :] = weighted


def attend(state, tables, queries, blocks, last=False):
    row_count, width = queries.shape
    plan = tuple((kind, which) for kind, which, _ in blocks)
    arrays = [array for _, _, group in blocks for array in group]
    first = state is None
    operands = [*tables, queries, *arrays, *(() if first else state)]
    whole = pl.BlockSpec(memory_space=pltpu.VMEM)
    if last:
        out_shape = jax.ShapeDtypeStruct((row_count, width), jnp.float32)
    else:
        out_shape = (
            jax.ShapeDtypeStruct((row_count, lane_count), jnp.float32),
            jax.ShapeDtypeStruct((row_count, lane_count), jnp.float32),
            jax.ShapeDtypeStruct((row_count, 2 * width), jnp.float32),
        )
    work = len(blocks) * row_count * row_count
    return pl.pallas_call(
        functools.partial(attend_kernel, plan, first, last),
        in_specs=[pl.BlockSpec(memory_space=pltpu.SMEM)] * 2 + [whole] * (len(operands) - 2),
        out_specs=whole if last else (whole,) * 3,
        out_shape=out_shape,
        compiler_params=pltpu.CompilerParams(vmem_limit_bytes=kernel_vmem),
        cost_estimate=pl.CostEstimate(
            flops=16 * work * width, bytes_accessed=8 * len(blocks) * row_count * width, transcendentals=work
        ),
    )(*operands)


def attend_all(state, tables, queries, blocks, last=False):
    for start in range(0, len(blocks), call_blocks):
        part = blocks[start : start + call_blocks]
        state = attend(state, tables, queries, part, last and start + call_blocks >= len(blocks))
    return state


def matching(size, distance, parity):
    lower = [i for i in range(size - distance) if (i // distance) % 2 == parity]
    return [(i, i + distance) for i in lower] + [(i + distance, i) for i in lower]


def attention(queries, keys, values, block_mask, partner_flags):
    blocks = lax.axis_size("space")
    groups = lax.axis_size("frame")
    levels = partner_flags.shape[1]
    tables = (block_mask, partner_flags)

    near = {}
    for parity in (1, 0):
        route = matching(groups, 1, parity)
        if route:
            near[parity] = (lax.ppermute(keys, "frame", route), lax.ppermute(values, "frame", route))
    near_blocks = [("pair", (("frame", 1, parity),), arrays) for parity, arrays in near.items()]

    far = {}
    if levels > 1:
        for parity in (1, 0):
            other = 1 - parity
            if other not in near:
                continue
            holders = {target for _, target in matching(groups, 1, other)}
            route = [pair for pair in matching(groups, 1, parity) if pair[0] in holders]
            if route:
                far[parity] = (
                    lax.ppermute(near[other][0], "frame", route), lax.ppermute(near[other][1], "frame", route)
                )
    far_blocks = [("pair", (("relay", 2, parity),), arrays) for parity, arrays in far.items()]
    if len(far_blocks) == 2 and groups <= 4:
        (_, (one,), here), (_, (two,), there) = far_blocks
        far_blocks = [("either", (one, two), (*here, *there))]
    for level in range(2, levels):
        for parity in (0, 1):
            route = matching(groups, 2**level, parity)
            if route:
                arrays = tuple(lax.ppermute(array, "frame", route) for array in (keys, values))
                far_blocks.append(("pair", (("frame", 2**level, parity),), arrays))

    window_blocks = []
    half = blocks // 2
    if half:
        route = matching(blocks, half, 0)
        arrays = (lax.ppermute(keys, "space", route), lax.ppermute(values, "space", route))
        window_blocks.append(("pair", (("space", half, 0),), arrays))
    side_blocks = []
    stacked = jnp.concatenate([keys, values], axis=0)
    for distance in range(half - 1, 0, -1):
        for parity in (0, 1):
            route = matching(blocks, distance, parity)
            if route:
                array = lax.ppermute(stacked, "space", route)
                side_blocks.append(("stacked", (("space", distance, parity),), (array,)))

    state = attend(None, tables, queries, [("pair", None, (keys, values))])
    state = attend_all(state, tables, queries, near_blocks + window_blocks + side_blocks[:1])
    state = attend_all(state, tables, queries, side_blocks[1:])
    return attend_all(state, tables, queries, far_blocks, last=True)


def solution(mesh):
    rows = P(("groups", "frame", "space"), None)
    return jax.shard_map(attention, mesh=mesh, in_specs=(rows, rows, rows, P(), P()), out_specs=rows, check_vma=False)
```

```python
import functools
import math

import jax
import jax.numpy as jnp
from jax import lax
from jax.experimental import pallas as pl
from jax.experimental.pallas import tpu as pltpu
from jax.sharding import PartitionSpec as P


masked_score = -1e30
lane_count = 128
row_chunk = 256
call_blocks = 4
kernel_vmem = 24 * 2**20
fetch_pieces = 4
far_distance = 2


def halves(x):
    high = x.astype(jnp.bfloat16)
    return high, (x - high.astype(jnp.float32)).astype(jnp.bfloat16)


def fold_lanes(x, op):
    folded = x[:, :lane_count]
    for start in range(lane_count, x.shape[1], lane_count):
        folded = op(folded, x[:, start : start + lane_count])
    return folded


def absorb(state, query_parts, key_parts, value_parts, enabled):
    scores = lax.dot_general(
        query_parts, key_parts, (((1,), (1,)), ((), ())), preferred_element_type=jnp.float32
    )
    block_max = jnp.max(fold_lanes(scores, jnp.maximum), axis=1, keepdims=True)
    if enabled is not None:
        block_max = chosen(enabled, block_max, jnp.full_like(block_max, masked_score))
    new_max = block_max if state is None else jnp.maximum(state[0], block_max)
    shift = new_max if enabled is None else chosen(enabled, new_max, jnp.full_like(new_max, -masked_score))
    weights = jnp.exp2(scores - shift)
    total = fold_lanes(weights, jnp.add)
    weights_high, weights_low = halves(weights)
    weighted = jnp.dot(weights_high, value_parts, preferred_element_type=jnp.float32)
    weighted += jnp.dot(weights_low, value_parts, preferred_element_type=jnp.float32)
    if state is None:
        return new_max, total, weighted
    factor = jnp.exp2(state[0] - new_max)
    return new_max, state[1] * factor + total, state[2] * factor + weighted


def partner_of(index, distance, parity):
    return jnp.where((index // distance) % 2 == parity, index + distance, index - distance)


def entry_of(entries, column):
    columns = lax.broadcasted_iota(jnp.int32, entries.shape, 1)
    return jnp.sum(jnp.where(columns == column, entries, 0).astype(jnp.float32), axis=1, keepdims=True)


def block_flag(which, block_mask, partner_flags):
    axis, distance, parity = which
    if axis == "space":
        index = lax.axis_index("space")
        return entry_of(block_mask[pl.ds(index, 1), :], partner_of(index, distance, parity))
    index = lax.axis_index("frame")
    if axis == "relay":
        partner = jnp.where(index % 2 == parity, index + distance, index - distance)
    else:
        partner = partner_of(index, distance, parity)
    inside = (partner >= 0) & (partner < lax.axis_size("frame"))
    upper = jnp.where(partner > index, 1, 0)
    entries = partner_flags[distance.bit_length() - 1, pl.ds(upper, 1), :]
    return entry_of(entries, jnp.where(inside, index, -1))


def chosen(flag, one, other):
    return jnp.where(jnp.broadcast_to(flag, one.shape) > 0, one, other)


def key_matrix(key_rows):
    key_high, key_low = halves(key_rows)
    return jnp.concatenate([key_high, key_high, key_low, key_low], axis=1)


def value_matrix(value_rows):
    return jnp.concatenate(halves(value_rows), axis=1)


def query_matrix(query_rows):
    score_scale = math.log2(math.e) / math.sqrt(query_rows.shape[1])
    query_high, query_low = halves(query_rows * score_scale)
    return jnp.concatenate([query_high, query_low, query_high, query_low], axis=1)


def rows_of(kind, refs):
    if kind == "stacked":
        rows = refs[0].shape[0] // 2
        return refs[0][:rows, :], refs[0][rows:, :], 1
    return refs[0][...], refs[1][...], 2


def read_block(kind, which, tables, refs):
    if kind != "either":
        key_rows, value_rows, used = rows_of(kind, refs)
        return key_rows, value_rows, block_flag(which, *tables), used
    position = 0
    key_rows = None
    for one_kind, one in which:
        more_keys, more_values, used = rows_of(one_kind, refs[position:])
        other = block_flag(one, *tables)
        if key_rows is None:
            key_rows, value_rows, flag = more_keys, more_values, other
        else:
            key_rows = chosen(other, more_keys, key_rows)
            value_rows = chosen(other, more_values, value_rows)
            flag = jnp.maximum(flag, other)
        position += used
    return key_rows, value_rows, flag, position


def own_kernel(queries, keys, values, out_max, out_total, out_weighted, stacked, query_parts, staged, sems):
    row_count = queries.shape[0]
    rows = keys.shape[0]
    copies = []
    for source, target, base in ((keys, stacked, 0), (queries, staged, 0), (values, stacked, rows)):
        piece = source.shape[0] // fetch_pieces
        for start in range(0, source.shape[0], piece):
            copy = pltpu.make_async_copy(
                source.at[start : start + piece, :],
                target.at[base + start : base + start + piece, :],
                sems.at[len(copies)],
            )
            copy.start()
            copies.append(copy)
    for copy in copies[: 2 * fetch_pieces]:
        copy.wait()
    key_parts = key_matrix(stacked[:rows, :])
    query_parts[...] = query_matrix(staged[...])
    for copy in copies[2 * fetch_pieces :]:
        copy.wait()
    value_parts = value_matrix(stacked[rows:, :])
    chunk = min(row_chunk, row_count)
    for start in range(0, row_count, chunk):
        part = slice(start, start + chunk)
        running_max, total, weighted = absorb(None, query_parts[part, :], key_parts, value_parts, None)
        out_max[part, :] = jnp.broadcast_to(running_max, (chunk, lane_count))
        out_total[part, :] = total
        out_weighted[part, :] = weighted


def attend_kernel(plan, last, block_mask, partner_flags, query_parts, *refs):
    position = 0
    key_parts = []
    value_parts = []
    enabled = []
    for kind, which in plan:
        key_rows, value_rows, flag, used = read_block(
            kind, which, (block_mask, partner_flags), refs[position:]
        )
        position += used
        key_parts.append(key_matrix(key_rows))
        value_parts.append(value_matrix(value_rows))
        enabled.append(flag)
    carried = refs[position : position + 3]
    outs = refs[position + 3 :]
    row_count = query_parts.shape[0]
    width = carried[2].shape[1] // 2
    chunk = min(row_chunk, row_count)
    copies = []
    for start in range(0, row_count, chunk):
        rows = slice(start, start + chunk)
        state = (carried[0][rows, :1], carried[1][rows, :], carried[2][rows, :])
        for index in range(len(plan)):
            state = absorb(state, query_parts[rows, :], key_parts[index], value_parts[index], enabled[index])
        running_max, total, weighted = state
        if last:
            out, staged, sems = outs
            inverse = 1.0 / jnp.sum(total, axis=1, keepdims=True)
            staged[rows, :] = (weighted[:, :width] + weighted[:, width:]) * inverse
            copy = pltpu.make_async_copy(staged.at[rows, :], out.at[rows, :], sems.at[len(copies)])
            copy.start()
            copies.append(copy)
        else:
            outs[0][rows, :] = jnp.broadcast_to(running_max, (chunk, lane_count))
            outs[1][rows, :] = total
            outs[2][rows, :] = weighted
    for copy in copies:
        copy.wait()


def cost_of(block_count, row_count, width):
    work = block_count * row_count * row_count
    return pl.CostEstimate(
        flops=16 * work * width, bytes_accessed=8 * block_count * row_count * width, transcendentals=work
    )


def state_shapes(row_count, width):
    return tuple(
        jax.ShapeDtypeStruct((row_count, columns), jnp.float32)
        for columns in (lane_count, lane_count, 2 * width)
    )


def attend_own(queries, keys, values):
    row_count, width = queries.shape
    whole = pl.BlockSpec(memory_space=pltpu.VMEM)
    operands = [pltpu.with_memory_space_constraint(array, pltpu.HBM) for array in (queries, keys, values)]
    out_shape = (
        *state_shapes(row_count, width),
        jax.ShapeDtypeStruct((2 * keys.shape[0], width), jnp.float32),
        jax.ShapeDtypeStruct((row_count, 4 * width), jnp.bfloat16),
    )
    *state, stacked, query_parts = pl.pallas_call(
        own_kernel,
        in_specs=[pl.BlockSpec(memory_space=pltpu.HBM)] * 3,
        out_specs=(whole,) * len(out_shape),
        out_shape=out_shape,
        scratch_shapes=[
            pltpu.VMEM((row_count, width), jnp.float32),
            pltpu.SemaphoreType.DMA((3 * fetch_pieces,)),
        ],
        compiler_params=pltpu.CompilerParams(vmem_limit_bytes=kernel_vmem),
        cost_estimate=cost_of(1, row_count, width),
    )(*operands)
    return state, stacked, query_parts


def attend(state, tables, query_parts, blocks, last=False):
    row_count = query_parts.shape[0]
    width = state[2].shape[1] // 2
    plan = tuple((kind, which) for kind, which, _ in blocks)
    arrays = [array for _, _, group in blocks for array in group]
    whole = pl.BlockSpec(memory_space=pltpu.VMEM)
    if last:
        out_shape = jax.ShapeDtypeStruct((row_count, width), jnp.float32)
        out_specs = pl.BlockSpec(memory_space=pl.ANY)
        pieces = row_count // min(row_chunk, row_count)
        scratch = [pltpu.VMEM((row_count, width), jnp.float32), pltpu.SemaphoreType.DMA((pieces,))]
    else:
        out_shape = state_shapes(row_count, width)
        out_specs = (whole,) * len(out_shape)
        scratch = []
    operands = (*tables, query_parts, *arrays, *state)
    return pl.pallas_call(
        functools.partial(attend_kernel, plan, last),
        in_specs=[whole] * len(operands),
        out_specs=out_specs,
        out_shape=out_shape,
        scratch_shapes=scratch,
        compiler_params=pltpu.CompilerParams(vmem_limit_bytes=kernel_vmem),
        cost_estimate=cost_of(len(blocks), row_count, width),
    )(*operands)


def attend_all(state, tables, query_parts, blocks):
    for start in range(0, len(blocks), call_blocks):
        state = attend(state, tables, query_parts, blocks[start : start + call_blocks])
    return state


def matching(size, distance, parity):
    lower = [i for i in range(size - distance) if (i // distance) % 2 == parity]
    return [(i, i + distance) for i in lower] + [(i + distance, i) for i in lower]


def attention(queries, keys, values, block_mask, partner_flags):
    blocks = lax.axis_size("space")
    groups = lax.axis_size("frame")
    levels = partner_flags.shape[1]
    tables = (block_mask, jnp.transpose(partner_flags, (1, 2, 0)))

    near = {}
    for parity in (1, 0):
        route = matching(groups, 1, parity)
        if route:
            near[parity] = (lax.ppermute(keys, "frame", route), lax.ppermute(values, "frame", route))
    near_blocks = [("pair", ("frame", 1, parity), arrays) for parity, arrays in near.items()]

    far_blocks = []
    for parity in (1, 0) if levels > 1 and len(near) == 2 else ():
        holders = {target for _, target in matching(groups, 1, 1 - parity)}
        route = [pair for pair in matching(groups, 1, parity) if pair[0] in holders]
        arrays = (lax.ppermute(near[1 - parity][0], "frame", route), lax.ppermute(near[1 - parity][1], "frame", route))
        far_blocks.append(("pair", ("relay", 2, parity), arrays))

    for level in range(2, levels):
        for parity in (0, 1):
            route = matching(groups, 2**level, parity)
            if route:
                arrays = tuple(lax.ppermute(array, "frame", route) for array in (keys, values))
                far_blocks.append(("pair", ("frame", 2**level, parity), arrays))

    state, stacked, query_parts = attend_own(queries, keys, values)

    window_blocks = []
    for distance in range(1, blocks // 2 + 1):
        for parity in (0, 1):
            route = matching(blocks, distance, parity)
            if route:
                array = lax.ppermute(stacked, "space", route)
                window_blocks.append(("stacked", ("space", distance, parity), (array,)))

    single = len(far_blocks) == 2 and groups <= 2 * far_distance
    final = far_blocks if single else (near_blocks + far_blocks)[-1:]
    sides = [block for block in window_blocks if block[1][2] == 0 and block[1][1] * 2 < blocks]
    rest = [block for block in window_blocks if all(block is not side for side in sides)]
    near_blocks = [block for block in near_blocks if all(block is not other for other in final)]
    far_blocks = [block for block in far_blocks if all(block is not other for other in final)]
    state = attend_all(state, tables, query_parts, sides + near_blocks)
    state = attend_all(state, tables, query_parts, rest)
    state = attend_all(state, tables, query_parts, far_blocks)
    if len(final) > 1:
        which = tuple((kind, one) for kind, one, _ in final)
        final = [("either", which, tuple(array for _, _, group in final for array in group))]
    return attend(state, tables, query_parts, final, last=True)


def solution(mesh):
    rows = P(("groups", "frame", "space"), None)
    return jax.shard_map(attention, mesh=mesh, in_specs=(rows, rows, rows, P(), P()), out_specs=rows, check_vma=False)
```

```python
import functools
import math

import jax
import jax.numpy as jnp
from jax import lax
from jax.experimental import pallas as pl
from jax.experimental.pallas import tpu as pltpu
from jax.sharding import PartitionSpec as P


masked_score = -1e30
lane_count = 128
row_chunk = 256
call_blocks = 4
kernel_vmem = 24 * 2**20
fetch_pieces = 4
write_pieces = 4
far_distance = 2


def halves(x):
    high = x.astype(jnp.bfloat16)
    return high, (x - high.astype(jnp.float32)).astype(jnp.bfloat16)


def fold_lanes(x, op):
    folded = x[:, :lane_count]
    for start in range(lane_count, x.shape[1], lane_count):
        folded = op(folded, x[:, start : start + lane_count])
    return folded


def absorb(state, query_parts, key_parts, value_parts, enabled):
    scores = lax.dot_general(
        query_parts, key_parts, (((1,), (1,)), ((), ())), preferred_element_type=jnp.float32
    )
    block_max = jnp.max(fold_lanes(scores, jnp.maximum), axis=1, keepdims=True)
    if enabled is not None:
        block_max = chosen(enabled, block_max, jnp.full_like(block_max, masked_score))
    new_max = block_max if state is None else jnp.maximum(state[0], block_max)
    shift = new_max if enabled is None else chosen(enabled, new_max, jnp.full_like(new_max, -masked_score))
    weights = jnp.exp2(scores - shift)
    total = fold_lanes(weights, jnp.add)
    weights_high, weights_low = halves(weights)
    weighted = jnp.dot(weights_high, value_parts, preferred_element_type=jnp.float32)
    weighted += jnp.dot(weights_low, value_parts, preferred_element_type=jnp.float32)
    if state is None:
        return new_max, total, weighted
    factor = jnp.exp2(state[0] - new_max)
    return new_max, state[1] * factor + total, state[2] * factor + weighted


def partner_of(index, distance, parity):
    return jnp.where((index // distance) % 2 == parity, index + distance, index - distance)


def entry_of(entries, column):
    columns = lax.broadcasted_iota(jnp.int32, entries.shape, 1)
    return jnp.sum(jnp.where(columns == column, entries, 0).astype(jnp.float32), axis=1, keepdims=True)


def block_flag(which, block_mask, partner_flags):
    axis, distance, parity = which
    if axis == "space":
        index = lax.axis_index("space")
        return entry_of(block_mask[pl.ds(index, 1), :], partner_of(index, distance, parity))
    index = lax.axis_index("frame")
    if axis == "relay":
        partner = jnp.where(index % 2 == parity, index + distance, index - distance)
    else:
        partner = partner_of(index, distance, parity)
    inside = (partner >= 0) & (partner < lax.axis_size("frame"))
    upper = jnp.where(partner > index, 1, 0)
    entries = partner_flags[distance.bit_length() - 1, pl.ds(upper, 1), :]
    return entry_of(entries, jnp.where(inside, index, -1))


def chosen(flag, one, other):
    return jnp.where(jnp.broadcast_to(flag, one.shape) > 0, one, other)


def key_matrix(key_rows):
    key_high, key_low = halves(key_rows)
    return jnp.concatenate([key_high, key_high, key_low, key_low], axis=1)


def value_matrix(value_rows):
    return jnp.concatenate(halves(value_rows), axis=1)


def query_matrix(query_rows):
    score_scale = math.log2(math.e) / math.sqrt(query_rows.shape[1])
    query_high, query_low = halves(query_rows * score_scale)
    return jnp.concatenate([query_high, query_low, query_high, query_low], axis=1)


def fetch_kernel(block_mask, partner_flags, queries, keys, values, stacked, query_copy, mask_copy, flags_copy, sems):
    rows = keys.shape[0]
    copies = []
    for source, target, base in ((keys, stacked, 0), (values, stacked, rows), (queries, query_copy, 0)):
        piece = source.shape[0] // fetch_pieces
        for start in range(0, source.shape[0], piece):
            copies.append(
                pltpu.make_async_copy(
                    source.at[start : start + piece, :],
                    target.at[base + start : base + start + piece, :],
                    sems.at[len(copies)],
                )
            )
    for source, target in ((block_mask, mask_copy), (partner_flags, flags_copy)):
        copies.append(pltpu.make_async_copy(source, target, sems.at[len(copies)]))
    for copy in copies:
        copy.start()
    for copy in copies:
        copy.wait()


def own_kernel(queries, stacked, out_max, out_total, out_weighted, query_parts):
    row_count = queries.shape[0]
    rows = stacked.shape[0] // 2
    key_parts = key_matrix(stacked[:rows, :])
    value_parts = value_matrix(stacked[rows:, :])
    chunk = min(row_chunk, row_count)
    for start in range(0, row_count, chunk):
        part = slice(start, start + chunk)
        query_chunk = query_matrix(queries[part, :])
        query_parts[part, :] = query_chunk
        running_max, total, weighted = absorb(None, query_chunk, key_parts, value_parts, None)
        out_max[part, :] = jnp.broadcast_to(running_max, (chunk, lane_count))
        out_total[part, :] = total
        out_weighted[part, :] = weighted


def read_blocks(plan, refs, tables):
    position = 0
    parts = []
    for kind, which in plan:
        if kind == "stacked":
            rows = refs[position].shape[0] // 2
            key_rows, value_rows = refs[position][:rows, :], refs[position][rows:, :]
            position += 1
        else:
            key_rows, value_rows = refs[position][...], refs[position + 1][...]
            position += 2
        parts.append((key_matrix(key_rows), value_matrix(value_rows), block_flag(which, *tables)))
    return parts, position


def attend_kernel(plan, block_mask, partner_flags, query_parts, *refs):
    parts, position = read_blocks(plan, refs, (block_mask, partner_flags))
    old_max, old_total, old_weighted, out_max, out_total, out_weighted = refs[position:]
    row_count = query_parts.shape[0]
    chunk = min(row_chunk, row_count)
    for start in range(0, row_count, chunk):
        rows = slice(start, start + chunk)
        state = (old_max[rows, :1], old_total[rows, :], old_weighted[rows, :])
        for part in parts:
            state = absorb(state, query_parts[rows, :], *part)
        running_max, total, weighted = state
        out_max[rows, :] = jnp.broadcast_to(running_max, (chunk, lane_count))
        out_total[rows, :] = total
        out_weighted[rows, :] = weighted


def brought(whiches, arrays, tables):
    rows = arrays[0][...]
    flag = block_flag(whiches[0], *tables)
    for which, array in zip(whiches[1:], arrays[1:]):
        other = block_flag(which, *tables)
        rows = chosen(other, array[...], rows)
        flag = jnp.maximum(flag, other)
    return rows, flag


def weigh_kernel(plan, whiches, block_mask, partner_flags, query_parts, *refs):
    tables = (block_mask, partner_flags)
    parts, position = read_blocks(plan, refs, tables)
    refs = refs[position:]
    count = len(whiches)
    key_rows, flag = brought(whiches, refs[:count], tables)
    old_max, old_total, old_weighted, out_high, out_low, out_inverse, out_weighted = refs[count:]
    key_parts = key_matrix(key_rows)
    row_count = query_parts.shape[0]
    width = key_rows.shape[1]
    chunk = min(row_chunk, row_count)
    for start in range(0, row_count, chunk):
        rows = slice(start, start + chunk)
        state = (old_max[rows, :1], old_total[rows, :], old_weighted[rows, :])
        for part in parts:
            state = absorb(state, query_parts[rows, :], *part)
        before, total, weighted = state
        scores = lax.dot_general(
            query_parts[rows, :],
            key_parts,
            (((1,), (1,)), ((), ())),
            preferred_element_type=jnp.float32,
        )
        block_max = jnp.max(fold_lanes(scores, jnp.maximum), axis=1, keepdims=True)
        block_max = chosen(flag, block_max, jnp.full_like(block_max, masked_score))
        new_max = jnp.maximum(before, block_max)
        factor = jnp.exp2(before - new_max)
        weights = jnp.exp2(scores - chosen(flag, new_max, jnp.full_like(new_max, -masked_score)))
        total = total * factor + fold_lanes(weights, jnp.add)
        inverse = 1.0 / jnp.sum(total, axis=1, keepdims=True)
        out_high[rows, :], out_low[rows, :] = halves(weights)
        out_inverse[rows, :] = jnp.broadcast_to(inverse, (chunk, lane_count))
        out_weighted[rows, :] = (weighted[:, :width] + weighted[:, width:]) * (factor * inverse)


def finish_kernel(whiches, block_mask, partner_flags, *refs):
    count = len(whiches)
    value_rows, _ = brought(whiches, refs[:count], (block_mask, partner_flags))
    weights_high, weights_low, inverse, weighted, out, staged, sems = refs[count:]
    value_parts = value_matrix(value_rows)
    row_count, width = weighted.shape
    chunk = row_count // write_pieces
    copies = []
    for start in range(0, row_count, chunk):
        rows = slice(start, start + chunk)
        more = jnp.dot(weights_high[rows, :], value_parts, preferred_element_type=jnp.float32)
        more += jnp.dot(weights_low[rows, :], value_parts, preferred_element_type=jnp.float32)
        staged[rows, :] = weighted[rows, :] + (more[:, :width] + more[:, width:]) * inverse[rows, :]
        copy = pltpu.make_async_copy(staged.at[rows, :], out.at[rows, :], sems.at[len(copies)])
        copy.start()
        copies.append(copy)
    for copy in copies:
        copy.wait()


def cost_of(block_count, row_count, width):
    work = block_count * row_count * row_count
    return pl.CostEstimate(
        flops=16 * work * width, bytes_accessed=8 * block_count * row_count * width, transcendentals=work
    )


def state_shapes(row_count, width):
    return tuple(
        jax.ShapeDtypeStruct((row_count, columns), jnp.float32)
        for columns in (lane_count, lane_count, 2 * width)
    )


def fetch(tables, queries, keys, values):
    rows, width = keys.shape
    whole = pl.BlockSpec(memory_space=pltpu.VMEM)
    operands = [
        pltpu.with_memory_space_constraint(array, pltpu.HBM) for array in (*tables, queries, keys, values)
    ]
    out_shape = (
        jax.ShapeDtypeStruct((2 * rows, width), keys.dtype),
        jax.ShapeDtypeStruct(queries.shape, queries.dtype),
        *(jax.ShapeDtypeStruct(table.shape, table.dtype) for table in tables),
    )
    stacked, query_copy, *tables = pl.pallas_call(
        fetch_kernel,
        in_specs=[pl.BlockSpec(memory_space=pltpu.HBM)] * len(operands),
        out_specs=(whole,) * len(out_shape),
        out_shape=out_shape,
        scratch_shapes=[pltpu.SemaphoreType.DMA((3 * fetch_pieces + len(tables),))],
        compiler_params=pltpu.CompilerParams(vmem_limit_bytes=kernel_vmem),
    )(*operands)
    return stacked, query_copy, tables


def attend_own(queries, stacked):
    row_count, width = queries.shape
    whole = pl.BlockSpec(memory_space=pltpu.VMEM)
    *state, query_parts = pl.pallas_call(
        own_kernel,
        in_specs=[whole] * 2,
        out_specs=(whole,) * 4,
        out_shape=(
            *state_shapes(row_count, width),
            jax.ShapeDtypeStruct((row_count, 4 * width), jnp.bfloat16),
        ),
        compiler_params=pltpu.CompilerParams(vmem_limit_bytes=kernel_vmem),
        cost_estimate=cost_of(1, row_count, width),
    )(queries, stacked)
    return state, query_parts


def attend(state, tables, query_parts, blocks):
    row_count = query_parts.shape[0]
    width = state[2].shape[1] // 2
    plan = tuple((kind, which) for kind, which, _ in blocks)
    arrays = [array for _, _, group in blocks for array in group]
    whole = pl.BlockSpec(memory_space=pltpu.VMEM)
    operands = (*tables, query_parts, *arrays, *state)
    return pl.pallas_call(
        functools.partial(attend_kernel, plan),
        in_specs=[whole] * len(operands),
        out_specs=(whole,) * 3,
        out_shape=state_shapes(row_count, width),
        compiler_params=pltpu.CompilerParams(vmem_limit_bytes=kernel_vmem),
        cost_estimate=cost_of(len(blocks), row_count, width),
    )(*operands)


def finish(state, tables, query_parts, others, blocks):
    row_count = query_parts.shape[0]
    width = state[2].shape[1] // 2
    whiches = tuple(which for _, which, _ in blocks)
    key_arrays = [keys for _, _, (keys, _) in blocks]
    value_arrays = [values for _, _, (_, values) in blocks]
    whole = pl.BlockSpec(memory_space=pltpu.VMEM)
    arrays = [array for _, _, group in others for array in group]
    plan = tuple((kind, which) for kind, which, _ in others)
    operands = (*tables, query_parts, *arrays, *key_arrays, *state)
    weights = jax.ShapeDtypeStruct((row_count, key_arrays[0].shape[0]), jnp.bfloat16)
    weighed = pl.pallas_call(
        functools.partial(weigh_kernel, plan, whiches),
        in_specs=[whole] * len(operands),
        out_specs=(whole,) * 4,
        out_shape=(
            weights,
            weights,
            jax.ShapeDtypeStruct((row_count, lane_count), jnp.float32),
            jax.ShapeDtypeStruct((row_count, width), jnp.float32),
        ),
        compiler_params=pltpu.CompilerParams(vmem_limit_bytes=kernel_vmem),
        cost_estimate=cost_of(1 + len(others), row_count, width),
    )(*operands)
    operands = (*tables, *value_arrays, *weighed)
    return pl.pallas_call(
        functools.partial(finish_kernel, whiches),
        in_specs=[whole] * len(operands),
        out_specs=pl.BlockSpec(memory_space=pl.ANY),
        out_shape=jax.ShapeDtypeStruct((row_count, width), jnp.float32),
        scratch_shapes=[
            pltpu.VMEM((row_count, width), jnp.float32),
            pltpu.SemaphoreType.DMA((write_pieces,)),
        ],
        compiler_params=pltpu.CompilerParams(vmem_limit_bytes=kernel_vmem),
        cost_estimate=cost_of(1, row_count, width),
    )(*operands)


def attend_all(state, tables, query_parts, blocks):
    for start in range(0, len(blocks), call_blocks):
        state = attend(state, tables, query_parts, blocks[start : start + call_blocks])
    return state


def matching(size, distance, parity):
    lower = [i for i in range(size - distance) if (i // distance) % 2 == parity]
    return [(i, i + distance) for i in lower] + [(i + distance, i) for i in lower]


def through_half(route, size):
    half = size // 2
    pairs = []
    for block, target in route:
        holder = block - half if block >= half else block + half
        if holder == target or abs(holder - target) > abs(block - target):
            return None
        pairs.append((holder, target))
    return pairs if len({holder for holder, _ in pairs}) == len(pairs) else None


def attention(queries, keys, values, block_mask, partner_flags):
    blocks = lax.axis_size("space")
    groups = lax.axis_size("frame")
    levels = partner_flags.shape[1]
    tables = (block_mask, jnp.transpose(partner_flags, (1, 2, 0)))

    near = {}
    for parity in (1, 0):
        route = matching(groups, 1, parity)
        if route:
            near[parity] = (lax.ppermute(keys, "frame", route), lax.ppermute(values, "frame", route))
    near_blocks = [("pair", ("frame", 1, parity), arrays) for parity, arrays in near.items()]

    far_blocks = []
    for parity in (1, 0) if levels > 1 and len(near) == 2 else ():
        holders = {target for _, target in matching(groups, 1, 1 - parity)}
        route = [pair for pair in matching(groups, 1, parity) if pair[0] in holders]
        arrays = (lax.ppermute(near[1 - parity][0], "frame", route), lax.ppermute(near[1 - parity][1], "frame", route))
        far_blocks.append(("pair", ("relay", 2, parity), arrays))

    for level in range(2, levels):
        for parity in (0, 1):
            route = matching(groups, 2**level, parity)
            if route:
                arrays = tuple(lax.ppermute(array, "frame", route) for array in (keys, values))
                far_blocks.append(("pair", ("frame", 2**level, parity), arrays))

    stacked, query_copy, tables = fetch(tables, queries, keys, values)
    state, query_parts = attend_own(query_copy, stacked)

    half = blocks // 2
    half_blocks = []
    early_blocks = []
    side_blocks = []
    for distance in range(half, 0, -1):
        for parity in (0, 1):
            route = matching(blocks, distance, parity)
            if not route:
                continue
            which = ("space", distance, parity)
            if distance == half:
                halved = lax.ppermute(stacked, "space", route)
                half_blocks.append(("stacked", which, (halved,)))
                continue
            source = stacked
            nearer = through_half(route, blocks) if parity else None
            if nearer:
                route, source = nearer, halved
            array = lax.ppermute(source, "space", route)
            (side_blocks if parity else early_blocks).append(("stacked", which, (array,)))

    single = len(far_blocks) == 2 and groups <= 2 * far_distance
    final = far_blocks if single else (near_blocks + far_blocks)[-1:]
    near_blocks, far_blocks = (
        [block for block in group if all(block is not other for other in final)]
        for group in (near_blocks, far_blocks)
    )
    state = attend_all(state, tables, query_parts, near_blocks + early_blocks)
    state = attend_all(state, tables, query_parts, half_blocks)
    state = attend_all(state, tables, query_parts, side_blocks[1:] + far_blocks)
    return finish(state, tables, query_parts, side_blocks[:1], final)


def solution(mesh):
    rows = P(("groups", "frame", "space"), None)
    return jax.shard_map(attention, mesh=mesh, in_specs=(rows, rows, rows, P(), P()), out_specs=rows, check_vma=False)
```

```python
import functools
import math

import jax
import jax.numpy as jnp
from jax import lax
from jax.experimental import pallas as pl
from jax.experimental.pallas import tpu as pltpu
from jax.sharding import PartitionSpec as P


masked_score = -1e30
lane_count = 128
row_chunk = 256
call_blocks = 4
kernel_vmem = 24 * 2**20
fetch_pieces = 4
write_pieces = 4
far_distance = 2


def halves(x):
    high = x.astype(jnp.bfloat16)
    return high, (x - high.astype(jnp.float32)).astype(jnp.bfloat16)


def fold_lanes(x, op):
    folded = x[:, :lane_count]
    for start in range(lane_count, x.shape[1], lane_count):
        folded = op(folded, x[:, start : start + lane_count])
    return folded


def absorb(state, query_parts, key_parts, value_parts, enabled):
    scores = lax.dot_general(
        query_parts, key_parts, (((1,), (1,)), ((), ())), preferred_element_type=jnp.float32
    )
    block_max = jnp.max(fold_lanes(scores, jnp.maximum), axis=1, keepdims=True)
    if enabled is not None:
        block_max = chosen(enabled, block_max, jnp.full_like(block_max, masked_score))
    new_max = block_max if state is None else jnp.maximum(state[0], block_max)
    shift = new_max if enabled is None else chosen(enabled, new_max, jnp.full_like(new_max, -masked_score))
    weights = jnp.exp2(scores - shift)
    total = fold_lanes(weights, jnp.add)
    weights_high, weights_low = halves(weights)
    weighted = jnp.dot(weights_high, value_parts, preferred_element_type=jnp.float32)
    weighted += jnp.dot(weights_low, value_parts, preferred_element_type=jnp.float32)
    if state is None:
        return new_max, total, weighted
    factor = jnp.exp2(state[0] - new_max)
    return new_max, state[1] * factor + total, state[2] * factor + weighted


def partner_of(index, distance, parity):
    return jnp.where((index // distance) % 2 == parity, index + distance, index - distance)


def entry_of(entries, column):
    columns = lax.broadcasted_iota(jnp.int32, entries.shape, 1)
    return jnp.sum(jnp.where(columns == column, entries, 0).astype(jnp.float32), axis=1, keepdims=True)


def block_flag(which, block_mask, partner_flags):
    axis, distance, parity = which
    if axis == "space":
        index = lax.axis_index("space")
        return entry_of(block_mask[pl.ds(index, 1), :], partner_of(index, distance, parity))
    index = lax.axis_index("frame")
    if axis == "relay":
        partner = jnp.where(index % 2 == parity, index + distance, index - distance)
    else:
        partner = partner_of(index, distance, parity)
    inside = (partner >= 0) & (partner < lax.axis_size("frame"))
    upper = jnp.where(partner > index, 1, 0)
    entries = partner_flags[distance.bit_length() - 1, pl.ds(upper, 1), :]
    return entry_of(entries, jnp.where(inside, index, -1))


def chosen(flag, one, other):
    return jnp.where(jnp.broadcast_to(flag, one.shape) > 0, one, other)


def key_matrix(key_rows):
    key_high, key_low = halves(key_rows)
    return jnp.concatenate([key_high, key_high, key_low, key_low], axis=1)


def value_matrix(value_rows):
    return jnp.concatenate(halves(value_rows), axis=1)


def query_matrix(query_rows):
    score_scale = math.log2(math.e) / math.sqrt(query_rows.shape[1])
    query_high, query_low = halves(query_rows * score_scale)
    return jnp.concatenate([query_high, query_low, query_high, query_low], axis=1)


def fetch_kernel(block_mask, partner_flags, queries, keys, values, stacked, query_copy, mask_copy, flags_copy, sems):
    rows = keys.shape[0]
    copies = []
    for source, target, base in ((keys, stacked, 0), (values, stacked, rows), (queries, query_copy, 0)):
        piece = source.shape[0] // fetch_pieces
        for start in range(0, source.shape[0], piece):
            copies.append(
                pltpu.make_async_copy(
                    source.at[start : start + piece, :],
                    target.at[base + start : base + start + piece, :],
                    sems.at[len(copies)],
                )
            )
    for source, target in ((block_mask, mask_copy), (partner_flags, flags_copy)):
        copies.append(pltpu.make_async_copy(source, target, sems.at[len(copies)]))
    for copy in copies:
        copy.start()
    for copy in copies:
        copy.wait()


def own_kernel(queries, stacked, out_max, out_total, out_weighted, query_parts):
    row_count = queries.shape[0]
    rows = stacked.shape[0] // 2
    key_parts = key_matrix(stacked[:rows, :])
    value_parts = value_matrix(stacked[rows:, :])
    chunk = min(row_chunk, row_count)
    for start in range(0, row_count, chunk):
        part = slice(start, start + chunk)
        query_chunk = query_matrix(queries[part, :])
        query_parts[part, :] = query_chunk
        running_max, total, weighted = absorb(None, query_chunk, key_parts, value_parts, None)
        out_max[part, :] = jnp.broadcast_to(running_max, (chunk, lane_count))
        out_total[part, :] = total
        out_weighted[part, :] = weighted


def read_blocks(plan, refs, tables):
    position = 0
    parts = []
    for kind, which in plan:
        if kind == "stacked":
            rows = refs[position].shape[0] // 2
            key_rows, value_rows = refs[position][:rows, :], refs[position][rows:, :]
            position += 1
        else:
            key_rows, value_rows = refs[position][...], refs[position + 1][...]
            position += 2
        parts.append((key_matrix(key_rows), value_matrix(value_rows), block_flag(which, *tables)))
    return parts, position


def attend_kernel(plan, block_mask, partner_flags, query_parts, *refs):
    parts, position = read_blocks(plan, refs, (block_mask, partner_flags))
    old_max, old_total, old_weighted, out_max, out_total, out_weighted = refs[position:]
    row_count = query_parts.shape[0]
    chunk = min(row_chunk, row_count)
    for start in range(0, row_count, chunk):
        rows = slice(start, start + chunk)
        state = (old_max[rows, :1], old_total[rows, :], old_weighted[rows, :])
        for part in parts:
            state = absorb(state, query_parts[rows, :], *part)
        running_max, total, weighted = state
        out_max[rows, :] = jnp.broadcast_to(running_max, (chunk, lane_count))
        out_total[rows, :] = total
        out_weighted[rows, :] = weighted


def brought(whiches, arrays, tables):
    rows = arrays[0][...]
    flag = block_flag(whiches[0], *tables)
    for which, array in zip(whiches[1:], arrays[1:]):
        other = block_flag(which, *tables)
        rows = chosen(other, array[...], rows)
        flag = jnp.maximum(flag, other)
    return rows, flag


def weigh_kernel(plan, whiches, block_mask, partner_flags, query_parts, *refs):
    tables = (block_mask, partner_flags)
    parts, position = read_blocks(plan, refs, tables)
    refs = refs[position:]
    count = len(whiches)
    key_rows, flag = brought(whiches, refs[:count], tables)
    old_max, old_total, old_weighted, out_high, out_low, out_inverse, out_weighted = refs[count:]
    key_parts = key_matrix(key_rows)
    row_count = query_parts.shape[0]
    width = key_rows.shape[1]
    chunk = min(row_chunk, row_count)
    for start in range(0, row_count, chunk):
        rows = slice(start, start + chunk)
        state = (old_max[rows, :1], old_total[rows, :], old_weighted[rows, :])
        for part in parts:
            state = absorb(state, query_parts[rows, :], *part)
        before, total, weighted = state
        scores = lax.dot_general(
            query_parts[rows, :],
            key_parts,
            (((1,), (1,)), ((), ())),
            preferred_element_type=jnp.float32,
        )
        block_max = jnp.max(fold_lanes(scores, jnp.maximum), axis=1, keepdims=True)
        block_max = chosen(flag, block_max, jnp.full_like(block_max, masked_score))
        new_max = jnp.maximum(before, block_max)
        factor = jnp.exp2(before - new_max)
        weights = jnp.exp2(scores - chosen(flag, new_max, jnp.full_like(new_max, -masked_score)))
        total = total * factor + fold_lanes(weights, jnp.add)
        inverse = 1.0 / jnp.sum(total, axis=1, keepdims=True)
        out_high[rows, :], out_low[rows, :] = halves(weights)
        out_inverse[rows, :] = jnp.broadcast_to(inverse, (chunk, lane_count))
        out_weighted[rows, :] = (weighted[:, :width] + weighted[:, width:]) * (factor * inverse)


def finish_kernel(whiches, block_mask, partner_flags, *refs):
    count = len(whiches)
    value_rows, _ = brought(whiches, refs[:count], (block_mask, partner_flags))
    weights_high, weights_low, inverse, weighted, out, staged, sems = refs[count:]
    value_parts = value_matrix(value_rows)
    row_count, width = weighted.shape
    chunk = row_count // write_pieces
    copies = []
    for start in range(0, row_count, chunk):
        rows = slice(start, start + chunk)
        more = jnp.dot(weights_high[rows, :], value_parts, preferred_element_type=jnp.float32)
        more += jnp.dot(weights_low[rows, :], value_parts, preferred_element_type=jnp.float32)
        staged[rows, :] = weighted[rows, :] + (more[:, :width] + more[:, width:]) * inverse[rows, :]
        copy = pltpu.make_async_copy(staged.at[rows, :], out.at[rows, :], sems.at[len(copies)])
        copy.start()
        copies.append(copy)
    for copy in copies:
        copy.wait()


def cost_of(block_count, row_count, width):
    work = block_count * row_count * row_count
    return pl.CostEstimate(
        flops=16 * work * width, bytes_accessed=8 * block_count * row_count * width, transcendentals=work
    )


def state_shapes(row_count, width):
    return tuple(
        jax.ShapeDtypeStruct((row_count, columns), jnp.float32)
        for columns in (lane_count, lane_count, 2 * width)
    )


def fetch(tables, queries, keys, values):
    rows, width = keys.shape
    whole = pl.BlockSpec(memory_space=pltpu.VMEM)
    operands = [
        pltpu.with_memory_space_constraint(array, pltpu.HBM) for array in (*tables, queries, keys, values)
    ]
    out_shape = (
        jax.ShapeDtypeStruct((2 * rows, width), keys.dtype),
        jax.ShapeDtypeStruct(queries.shape, queries.dtype),
        *(jax.ShapeDtypeStruct(table.shape, table.dtype) for table in tables),
    )
    stacked, query_copy, *tables = pl.pallas_call(
        fetch_kernel,
        in_specs=[pl.BlockSpec(memory_space=pltpu.HBM)] * len(operands),
        out_specs=(whole,) * len(out_shape),
        out_shape=out_shape,
        scratch_shapes=[pltpu.SemaphoreType.DMA((3 * fetch_pieces + len(tables),))],
        compiler_params=pltpu.CompilerParams(vmem_limit_bytes=kernel_vmem),
    )(*operands)
    return stacked, query_copy, tables


def attend_own(queries, stacked):
    row_count, width = queries.shape
    whole = pl.BlockSpec(memory_space=pltpu.VMEM)
    *state, query_parts = pl.pallas_call(
        own_kernel,
        in_specs=[whole] * 2,
        out_specs=(whole,) * 4,
        out_shape=(
            *state_shapes(row_count, width),
            jax.ShapeDtypeStruct((row_count, 4 * width), jnp.bfloat16),
        ),
        compiler_params=pltpu.CompilerParams(vmem_limit_bytes=kernel_vmem),
        cost_estimate=cost_of(1, row_count, width),
    )(queries, stacked)
    return state, query_parts


def attend(state, tables, query_parts, blocks):
    row_count = query_parts.shape[0]
    width = state[2].shape[1] // 2
    plan = tuple((kind, which) for kind, which, _ in blocks)
    arrays = [array for _, _, group in blocks for array in group]
    whole = pl.BlockSpec(memory_space=pltpu.VMEM)
    operands = (*tables, query_parts, *arrays, *state)
    return pl.pallas_call(
        functools.partial(attend_kernel, plan),
        in_specs=[whole] * len(operands),
        out_specs=(whole,) * 3,
        out_shape=state_shapes(row_count, width),
        compiler_params=pltpu.CompilerParams(vmem_limit_bytes=kernel_vmem),
        cost_estimate=cost_of(len(blocks), row_count, width),
    )(*operands)


def finish(state, tables, query_parts, others, blocks):
    row_count = query_parts.shape[0]
    width = state[2].shape[1] // 2
    whiches = tuple(which for _, which, _ in blocks)
    key_arrays = [keys for _, _, (keys, _) in blocks]
    value_arrays = [values for _, _, (_, values) in blocks]
    whole = pl.BlockSpec(memory_space=pltpu.VMEM)
    arrays = [array for _, _, group in others for array in group]
    plan = tuple((kind, which) for kind, which, _ in others)
    operands = (*tables, query_parts, *arrays, *key_arrays, *state)
    weights = jax.ShapeDtypeStruct((row_count, key_arrays[0].shape[0]), jnp.bfloat16)
    weighed = pl.pallas_call(
        functools.partial(weigh_kernel, plan, whiches),
        in_specs=[whole] * len(operands),
        out_specs=(whole,) * 4,
        out_shape=(
            weights,
            weights,
            jax.ShapeDtypeStruct((row_count, lane_count), jnp.float32),
            jax.ShapeDtypeStruct((row_count, width), jnp.float32),
        ),
        compiler_params=pltpu.CompilerParams(vmem_limit_bytes=kernel_vmem),
        cost_estimate=cost_of(1 + len(others), row_count, width),
    )(*operands)
    operands = (*tables, *value_arrays, *weighed)
    return pl.pallas_call(
        functools.partial(finish_kernel, whiches),
        in_specs=[whole] * len(operands),
        out_specs=pl.BlockSpec(memory_space=pl.ANY),
        out_shape=jax.ShapeDtypeStruct((row_count, width), jnp.float32),
        scratch_shapes=[
            pltpu.VMEM((row_count, width), jnp.float32),
            pltpu.SemaphoreType.DMA((write_pieces,)),
        ],
        compiler_params=pltpu.CompilerParams(vmem_limit_bytes=kernel_vmem),
        cost_estimate=cost_of(1, row_count, width),
    )(*operands)


def attend_all(state, tables, query_parts, blocks):
    for start in range(0, len(blocks), call_blocks):
        state = attend(state, tables, query_parts, blocks[start : start + call_blocks])
    return state


def matching(size, distance, parity):
    lower = [i for i in range(size - distance) if (i // distance) % 2 == parity]
    return [(i, i + distance) for i in lower] + [(i + distance, i) for i in lower]


def both_ways(route):
    sources = {source for source, _ in route}
    targets = {target for _, target in route}
    return route + [(two, one) for one, two in route if two not in sources and one not in targets]


def moved_along_frames(array, route):
    blocks = lax.axis_size("space")
    left_out = set(range(lax.axis_size("frame"))) - {frame for pair in route for frame in pair}
    pairs = [(one * blocks + s, two * blocks + s) for one, two in route for s in range(blocks)]
    for frame in sorted(left_out):
        pairs += [(frame * blocks + one, frame * blocks + two) for one, two in matching(blocks, 1, 0)]
    return lax.ppermute(array, ("frame", "space"), pairs)


def through_half(route, size):
    half = size // 2
    pairs = []
    for block, target in route:
        holder = block - half if block >= half else block + half
        if holder == target or abs(holder - target) > abs(block - target):
            return None
        pairs.append((holder, target))
    return pairs if len({holder for holder, _ in pairs}) == len(pairs) else None


def attention(queries, keys, values, block_mask, partner_flags):
    blocks = lax.axis_size("space")
    groups = lax.axis_size("frame")
    levels = partner_flags.shape[1]
    tables = (block_mask, jnp.transpose(partner_flags, (1, 2, 0)))

    near = {}
    for parity in (1, 0):
        route = matching(groups, 1, parity)
        if route:
            near[parity] = (moved_along_frames(keys, route), moved_along_frames(values, route))
    near_blocks = [("pair", ("frame", 1, parity), arrays) for parity, arrays in near.items()]

    far_blocks = []
    for parity in (1, 0) if levels > 1 and len(near) == 2 else ():
        holders = {target for _, target in matching(groups, 1, 1 - parity)}
        route = [pair for pair in matching(groups, 1, parity) if pair[0] in holders]
        arrays = (moved_along_frames(near[1 - parity][0], route), moved_along_frames(near[1 - parity][1], route))
        far_blocks.append(("pair", ("relay", 2, parity), arrays))

    for level in range(2, levels):
        for parity in (0, 1):
            route = matching(groups, 2**level, parity)
            if route:
                arrays = tuple(lax.ppermute(array, "frame", route) for array in (keys, values))
                far_blocks.append(("pair", ("frame", 2**level, parity), arrays))

    stacked, query_copy, tables = fetch(tables, queries, keys, values)
    state, query_parts = attend_own(query_copy, stacked)

    half = blocks // 2
    half_blocks = []
    early_blocks = []
    side_blocks = []
    for distance in range(half, 0, -1):
        for parity in (0, 1):
            route = matching(blocks, distance, parity)
            if not route:
                continue
            which = ("space", distance, parity)
            if distance == half:
                halved = lax.ppermute(stacked, "space", route)
                half_blocks.append(("stacked", which, (halved,)))
                continue
            source = stacked
            nearer = through_half(route, blocks) if parity else None
            if nearer:
                route, source = both_ways(nearer), halved
            array = lax.ppermute(source, "space", route)
            (side_blocks if parity else early_blocks).append(("stacked", which, (array,)))

    single = len(far_blocks) == 2 and groups <= 2 * far_distance
    final = far_blocks if single else (near_blocks + far_blocks)[-1:]
    near_blocks, far_blocks = (
        [block for block in group if all(block is not other for other in final)]
        for group in (near_blocks, far_blocks)
    )
    state = attend_all(state, tables, query_parts, near_blocks + early_blocks + half_blocks)
    state = attend_all(state, tables, query_parts, side_blocks[1:] + far_blocks)
    return finish(state, tables, query_parts, side_blocks[:1], final)


def solution(mesh):
    rows = P(("groups", "frame", "space"), None)
    return jax.shard_map(attention, mesh=mesh, in_specs=(rows, rows, rows, P(), P()), out_specs=rows, check_vma=False)
```
